256 devices in a mesh: clu: 32 (over x, y, core), sub: 8 (over z).
Axes of the slice: x: 4, y: 4, z: 8, core: 2. Of those that a mesh axis runs over, the one named last changes fastest.
Arguments:
- load_cases: float32 [128, 393216], P(None, ('clu', 'sub')), may hold values from -90 to 90
- initial: float32 [128, 393216], P(None, ('clu', 'sub')), may hold values from -6 to 6
- dual_blocks: bfloat16 [393216, 1536], P(('clu', 'sub')), may hold values from -1 to 3, as said below
- dirichlet: bfloat16 [393216, 1536], P(('clu', 'sub')), may hold values from -1 to 3, as said below
- rigid_modes: float32 [16384, 1536], P(('clu', 'sub')), may hold values from -1 to 1
- coarse_inverse: float32 [16384, 512], P(('clu', 'sub')), may hold values from -2 to 2, as said below
- face_block: int32 [256, 12], P(('clu', 'sub')), may hold values from 0 to 11, each once within a row
- active: int32 [256, 4], P(('clu', 'sub')), may hold values from 0 to 1, as said below
- membership: int32 [256], P('clu'), may hold values from 0 to 1
Outputs:
- multipliers: float32 [128, 393216], P(None, ('clu', 'sub'))
- residual: float32 [128, 393216], P(None, ('clu', 'sub'))
The draws below stay inside these ranges and needn't reach their ends.
Inputs may be any that keep to these rules, and one draw needn't show every extreme that they name: active[s, g] equals active[p, g] for the partner p of subdomain s in colour g. `coarse_inverse`: each cluster's 512 rows form the inverse of the symmetric positive definite matrix C C^T + 0.5 I, where C stacks the rigid_modes rows of the cluster's subdomains. `dual_blocks`: each subdomain's block is symmetric. `dirichlet`: each subdomain's block is symmetric.
All inputs are finite; a program needn't handle non-finite values.
Results may differ from the reference program's by a relative error of at most 0.0022.
Values sent between devices are 32-bit elements; how exact they have to be, the bound alone decides.
No kernel may reach another device: no remote copies, remote signals or barrier semaphores. Data moves between devices by JAX's collectives and lax.ppermute only.
A program may use at most 64 MiB of HBM per device.

```python
import math
import jax
import jax.numpy as jnp
from jax import lax

M = 1536
BLK = 128
E = 64
K = 128
NCOL = 4
NGRP = 2
ITERS = 3
NB = 12
SLOTS = 3
CLUSTERS = 32
PER_CLU = 8
SUBDOMS = 256
CE = 512
MT = 393216


def symmetric_blocks(key):
    keys = jax.random.split(key, SUBDOMS)

    def single(one_key):
        first, second = jax.random.split(one_key)
        raw = jnp.clip(jax.random.normal(first, (M, M), jnp.float32), -5.0, 5.0)
        offdiag = (raw + raw.T) * (0.7 / math.sqrt(2.0 * M))
        diagonal = jnp.exp(jax.random.uniform(second, (M,), jnp.float32, math.log(0.5), math.log(2.0)))
        return (offdiag + jnp.diag(diagonal)).astype(jnp.bfloat16)
    return lax.map(single, keys).reshape(SUBDOMS * M, M)


def draw_dual_blocks(key, part):
    return symmetric_blocks(jax.random.fold_in(key, 11))


def draw_dirichlet(key, part):
    return symmetric_blocks(jax.random.fold_in(key, 23))


def mode_rows(key):
    raw = jnp.clip(jax.random.normal(jax.random.fold_in(key, 61), (SUBDOMS * E, M), jnp.float32), -5.0, 5.0)
    return raw * (2.0 / math.sqrt(M))


def draw_rigid_modes(key, part):
    return mode_rows(key)


def draw_coarse_inverse(key, part):
    modes = mode_rows(key).reshape(CLUSTERS, CE, M)

    def single(cluster_modes):
        gram = jnp.dot(cluster_modes, cluster_modes.T, precision=lax.Precision.HIGHEST)
        gram = gram + 0.5 * jnp.eye(CE, dtype=jnp.float32)
        inverse = jnp.linalg.inv(gram)
        return 0.5 * (inverse + inverse.T)
    return jnp.clip(lax.map(single, modes).reshape(SUBDOMS * E, CE), -2.0, 2.0)


def draw_load_cases(key, part):
    base_key = jax.random.fold_in(key, 41)
    first, second, third = jax.random.split(base_key, 3)
    base = jnp.clip(jax.random.normal(first, (K, MT), jnp.float32), -5.0, 5.0)
    row_scale = 0.3 * jnp.exp(jax.random.uniform(second, (K, 1), jnp.float32, 0.0, math.log(10.0)))
    col_scale = 0.3 * jnp.exp(jax.random.uniform(third, (1, MT), jnp.float32, 0.0, math.log(10.0)))
    trend = 0.6 * (1.0 + 2.0 * jnp.arange(MT, dtype=jnp.float32)[None, :] / (MT - 1))
    return jnp.clip(base * row_scale * col_scale * trend, -90.0, 90.0)


def draw_active(key, part):
    bits = (jax.random.randint(jax.random.fold_in(key, 53), (SUBDOMS, NCOL), 0, 4) != 0).astype(jnp.int32)
    index = jnp.arange(SUBDOMS, dtype=jnp.int32)
    cluster = index // PER_CLU
    inside = index % PER_CLU
    columns = []
    for colour in range(NCOL):
        if colour < NCOL - 1:
            partner = jnp.bitwise_xor(cluster, 1 << colour) * PER_CLU + inside
        else:
            partner = cluster * PER_CLU + jnp.bitwise_xor(inside, 1)
        lower = jnp.minimum(index, partner)
        columns.append(bits[lower, colour])
    return jnp.stack(columns, axis=1).astype(jnp.int32)


def place_ends(entries, key, least, top_value):
    longest = entries.shape.index(max(entries.shape))
    spots = []
    for shift in (0, 1):
        where = [jax.random.randint(jax.random.fold_in(key, axis), (), 0, length) for axis, length in enumerate(entries.shape)]
        where[longest] = (where[longest] + shift) % entries.shape[longest]
        spots.append(tuple(where))
    return entries.at[spots[0]].set(least).at[spots[1]].set(top_value)


def shard_levels(stream_key, dims, shards, smallest, largest):
    def one(position, blocks):
        steps = jax.random.uniform(jax.random.fold_in(jax.random.fold_in(stream_key, 6), position), (blocks,), jnp.float32, smallest / len(shards), largest / len(shards))
        return jnp.repeat(jnp.exp(steps), dims[position] // blocks).reshape((-1,) + (1,) * (len(dims) - position - 1))

    level = one(*shards[0])
    for cut in shards[1:]:
        level = level * one(*cut)
    return level


def centred(key, shape, spread, bound, cuts=(), held_as=jnp.bfloat16):
    values = jax.random.normal(key, shape, jnp.float32) * spread
    if len(cuts) > 0:
        values = shard_levels(key, shape, cuts, -0.22, 0.18) * values
    return jnp.clip(values, min=-bound, max=bound).astype(held_as)


def setup_inputs(seed: int = 0) -> dict:
    key_list = jax.random.split(jax.random.key(seed), 10)
    return {
        "load_cases": draw_load_cases(jax.random.fold_in(key_list[9], 71), 0),
        "initial": centred(key_list[1], (K, MT), 1.0, 6.0, ((1, 256),), jnp.float32),
        "dual_blocks": draw_dual_blocks(jax.random.fold_in(key_list[9], 71), 0),
        "dirichlet": draw_dirichlet(jax.random.fold_in(key_list[9], 71), 0),
        "rigid_modes": draw_rigid_modes(jax.random.fold_in(key_list[9], 71), 0),
        "coarse_inverse": draw_coarse_inverse(jax.random.fold_in(key_list[9], 71), 0),
        "face_block": jax.vmap(lambda own: jax.random.permutation(own, NB))(jax.random.split(key_list[6], SUBDOMS)).reshape((SUBDOMS, NB)).astype(jnp.int32),
        "active": draw_active(jax.random.fold_in(key_list[9], 71), 0),
        "membership": place_ends(jax.random.randint(key_list[8], (SUBDOMS,), 0, NGRP), jax.random.fold_in(key_list[8], 1), 0, NGRP - 1).astype(jnp.int32),
    }


HIGH = lax.Precision.HIGHEST

def by_subdomain(vector):
    return vector.reshape(K, SUBDOMS, M).transpose(1, 0, 2)

def by_case(vector):
    return vector.transpose(1, 0, 2).reshape(K, MT)

def apply_local(vector, blocks):
    stacked = blocks.reshape(SUBDOMS, M, M)

    def single(pair):
        return jnp.dot(pair[0].astype(jnp.bfloat16).astype(jnp.float32), pair[1].astype(jnp.float32), preferred_element_type=jnp.float32)
    return lax.map(single, (vector, stacked))

def assemble(product, face_block, active):
    onehot = (face_block[:, :, None] == jnp.arange(NB)[None, None, :]).astype(jnp.float32)
    blocked = product.reshape(SUBDOMS, K, NB, BLK)
    slot_vals = jnp.einsum('sjq,skqb->skjb', onehot, blocked, precision=HIGH)
    index = jnp.arange(SUBDOMS)
    cluster = index // PER_CLU
    inside = index % PER_CLU
    received = []
    for colour in range(NCOL):
        if colour < NCOL - 1:
            partner = jnp.bitwise_xor(cluster, 1 << colour) * PER_CLU + inside
        else:
            partner = cluster * PER_CLU + jnp.bitwise_xor(inside, 1)
        piece = slot_vals[partner][:, :, colour * SLOTS:(colour + 1) * SLOTS, :]
        received.append(piece * active[:, colour].astype(jnp.float32)[:, None, None, None])
    joined = jnp.concatenate(received, axis=2)
    added = jnp.einsum('sjq,skjb->skqb', onehot, joined, precision=HIGH)
    return product + added.reshape(SUBDOMS, K, M)

def coarse(vector, rigid_modes, coarse_inverse, membership):
    modes3 = rigid_modes.reshape(SUBDOMS, E, M)
    inverse3 = coarse_inverse.reshape(SUBDOMS, E, CE)
    coeffs = jnp.einsum('sem,skm->sek', modes3, vector, precision=HIGH)
    cluster = jnp.arange(SUBDOMS) // PER_CLU
    gathered = coeffs.reshape(CLUSTERS, CE, K)[cluster]
    groups = membership.reshape(CLUSTERS, PER_CLU)[cluster]
    same_group = (groups == membership[:, None]).astype(jnp.float32)
    widened = jnp.repeat(same_group, E, axis=1)
    amounts = jnp.einsum('sex,sxk->sek', inverse3, gathered * widened[:, :, None], precision=HIGH)
    correction = jnp.einsum('sem,sek->skm', modes3, amounts, precision=HIGH)
    return vector - correction

def reference(load_cases, initial, dual_blocks, dirichlet, rigid_modes, coarse_inverse, face_block, active, membership):
    start_vec = by_subdomain(initial)
    residual = coarse(by_subdomain(load_cases) - assemble(apply_local(start_vec, dual_blocks), face_block, active), rigid_modes, coarse_inverse, membership)
    multipliers = start_vec
    for step in range(ITERS):
        search = coarse(assemble(apply_local(residual, dirichlet), face_block, active), rigid_modes, coarse_inverse, membership)
        image = coarse(assemble(apply_local(search, dual_blocks), face_block, active), rigid_modes, coarse_inverse, membership)
        cross_sum = jnp.sum(residual * image, axis=(0, 2))
        image_sum = jnp.sum(image * image, axis=(0, 2))
        step_len = cross_sum / (image_sum + 1e-06)
        multipliers = multipliers + step_len[None, :, None] * search
        residual = residual - step_len[None, :, None] * image
    return (by_case(multipliers), by_case(residual))
```

```python
import functools

import jax
import jax.numpy as jnp
from jax import lax
from jax.experimental import pallas as pl
from jax.experimental.pallas import tpu as pltpu
from jax.sharding import PartitionSpec as P

BLK = 128
E = 64
K = 128
M = 1536
NB = 12
NCOL = 4
SLOTS = 3
FACE = SLOTS * BLK
ITERS = 3
PER_CLU = 8
CLU = 32
ROWS = 16
PAIRS = ((0, 1), (0, 2), (0, 3), (1, 1), (1, 2), (1, 3), (2, 2), (2, 3), (3, 3))


F32 = jnp.float32
BF16 = jnp.bfloat16
VMEM = pl.BlockSpec(memory_space=pltpu.VMEM)
SMEM = pl.BlockSpec(memory_space=pltpu.SMEM)


def call(body, outs, in_specs, scratch=(), limit=24, flops=0, moved=0):
    return pl.pallas_call(
        body,
        out_shape=outs,
        in_specs=in_specs,
        out_specs=[VMEM] * len(outs),
        scratch_shapes=list(scratch),
        compiler_params=pltpu.CompilerParams(vmem_limit_bytes=limit << 20),
        cost_estimate=pl.CostEstimate(flops=flops, bytes_accessed=moved, transcendentals=0),
    )


def split(x):
    hi = x.astype(BF16)
    return hi, (x - hi.astype(F32)).astype(BF16)


def dot(a, b):
    return jnp.dot(a, b, preferred_element_type=F32)


def three(out):
    return out[:E, :K] + out[:E, K:] + out[E:, :K]


def block(index):
    return pl.ds(pl.multiple_of(index * BLK, BLK), BLK)


def put_terms(terms, where, x):
    hi, lo = split(x)
    terms[where, :K] = hi
    terms[where, K:] = lo


def product(fb, op, terms, faces):
    for j in range(NB):
        out = dot(op[block(fb[0, j]), :], terms[...])
        lo = (j % SLOTS) * BLK
        faces[j // SLOTS][lo : lo + BLK, :] = out[:, :K] + out[:, K:]


def prep_body(fb, modes, inverse, stacked, correct, inv_terms):
    for j in range(NB):
        hi, lo = split(modes[:, block(fb[0, j])])
        cols = slice(j * BLK, (j + 1) * BLK)
        stacked[:E, cols] = hi
        stacked[E:, cols] = lo
        four = jnp.concatenate([hi, hi, lo, lo], axis=0)
        correct[cols, :] = four.astype(F32).T.astype(BF16)
    hi, lo = split(inverse[...])
    inv_terms[:E, :] = hi
    inv_terms[E:, :] = lo


def first_body(fb, start, op, f0, f1, f2, f3, terms):
    for i in range(NB):
        rows = slice(i * BLK, (i + 1) * BLK)
        put_terms(terms, rows, start[:, rows].T)
    product(fb, op, terms, (f0, f1, f2, f3))


def coeffs_out(terms, stacked, sent):
    coeffs = three(dot(stacked[...], terms[...]))
    for t in range(PER_CLU):
        sent[t] = coeffs


def gathered(gates, faces, rcvs, j):
    lo = (j % SLOTS) * BLK
    g = j // SLOTS
    return faces[g][lo : lo + BLK, :] + gates[0, g] * rcvs[g][lo : lo + BLK, :]


def asm_body(gates, f0, f1, f2, f3, r0, r1, r2, r3, stacked, w, sent, terms):
    for j in range(NB):
        rows = slice(j * BLK, (j + 1) * BLK)
        value = gathered(gates, (f0, f1, f2, f3), (r0, r1, r2, r3), j)
        w[rows, :] = value
        put_terms(terms, rows, value)
    coeffs_out(terms, stacked, sent)


def asm_first_body(fb, gates, f0, f1, f2, f3, r0, r1, r2, r3, stacked, load, w, sent, terms):
    for j in range(NB):
        rows = slice(j * BLK, (j + 1) * BLK)
        value = load[:, block(fb[0, j])].T - gathered(gates, (f0, f1, f2, f3), (r0, r1, r2, r3), j)
        w[rows, :] = value
        put_terms(terms, rows, value)
    coeffs_out(terms, stacked, sent)


def amounts(group, got, inv_terms, pieces):
    for t in range(PER_CLU):
        put_terms(pieces, slice(t * E, (t + 1) * E), got[t] * group[0, t])
    hi, lo = split(three(dot(inv_terms[...], pieces[...])))
    return jnp.concatenate([hi, lo, hi, lo], axis=0)


def mat_body(fb, group, w, got, inv_terms, correct, op, v, f0, f1, f2, f3, terms, pieces):
    z = amounts(group, got, inv_terms, pieces)
    for j in range(NB):
        rows = slice(j * BLK, (j + 1) * BLK)
        value = w[rows, :] - dot(correct[rows, :], z)
        v[rows, :] = value
        put_terms(terms, block(fb[0, j]), value)
    product(fb, op, terms, (f0, f1, f2, f3))


def gram_body(group, w, got, inv_terms, correct, k0, k1, k2, k3, sums, pieces):
    z = amounts(group, got, inv_terms, pieces)
    tops = [jnp.zeros((8, K), F32) for _ in range(4)]

    def octets(x):
        return x.reshape(BLK // 8, 8, K)

    for j in range(NB):
        rows = slice(j * BLK, (j + 1) * BLK)
        value = w[rows, :] - dot(correct[rows, :], z)
        k3[rows, :] = value
        basis = (k0[rows, :], k1[rows, :], k2[rows, :], value)
        tops = [jnp.maximum(t, jnp.max(octets(jnp.abs(x)), axis=0)) for t, x in zip(tops, basis)]
    tops = [jnp.max(t, axis=0, keepdims=True) for t in tops]
    scales = [jnp.where(t > 1e-37, 1.0 / t, 0.0) for t in tops]
    totals = [jnp.zeros((8, K), F32) for _ in PAIRS]
    for j in range(NB):
        rows = slice(j * BLK, (j + 1) * BLK)
        basis = [x[rows, :] * s for x, s in zip((k0, k1, k2, k3), scales)]
        totals = [t + jnp.sum(octets(basis[a] * basis[b]), axis=0) for t, (a, b) in zip(totals, PAIRS)]
    lines = tops + [jnp.sum(t, axis=0, keepdims=True) for t in totals]
    lines = lines + [jnp.zeros((1, K), F32)] * (ROWS - len(lines))
    table = jnp.concatenate(lines, axis=0)
    for t in range(CLU):
        sums[t] = table


def combine(parts, count):
    tables = [parts[t] for t in range(count)]
    top = functools.reduce(jnp.maximum, tables)[:4]
    scale = jnp.where(top > 1e-37, 1.0 / top, 0.0)
    total = [jnp.zeros((1, K), F32) for _ in PAIRS]
    for table in tables:
        part = table[:4] * scale
        total = [
            t + table[4 + i : 5 + i] * (part[a : a + 1] * part[b : b + 1])
            for i, (t, (a, b)) in enumerate(zip(total, PAIRS))
        ]
    return [top[i : i + 1] for i in range(4)], total


def combine_body(parts, sums):
    tops, totals = combine(parts, CLU)
    lines = tops + totals
    lines = lines + [jnp.zeros((1, K), F32)] * (ROWS - len(lines))
    table = jnp.concatenate(lines, axis=0)
    for t in range(PER_CLU):
        sums[t] = table


def last_body(fb, parts, start, t0, t1, t2, k0, k1, k2, k3, mult, resid):
    tops, totals = combine(parts, PER_CLU)
    gram = {}
    for total, (a, b) in zip(totals, PAIRS):
        gram[a, b] = gram[b, a] = total
    inv = [jnp.where(t > 1e-37, 1.0 / t, 0.0) for t in tops]
    ratio = [tops[j + 1] * inv[j] for j in range(3)]
    zero = jnp.zeros((1, K), F32)
    res = [tops[0], zero, zero, zero]
    mul = [zero, zero, zero]
    for i in range(ITERS):
        img = [zero] + [res[j] * ratio[j] for j in range(3)]
        cross, image = zero, zero
        for b in range(1, i + 2):
            for a in range(i + 1):
                cross = cross + (res[a] * img[b]) * gram[a, b]
            for a in range(1, i + 2):
                image = image + (img[a] * img[b]) * gram[a, b]
        step = cross / (image + 1e-06)
        mul = [m + step * (r * s) for m, r, s in zip(mul, res, inv)]
        res = [r - step * q for r, q in zip(res, img)]
    res = [r * s for r, s in zip(res, inv)]
    for j in range(NB):
        rows = slice(j * BLK, (j + 1) * BLK)
        cols = block(fb[0, j])
        gain = mul[0] * t0[rows, :] + mul[1] * t1[rows, :] + mul[2] * t2[rows, :]
        mult[:, cols] = start[:, cols] + gain.T
        left = res[0] * k0[rows, :] + res[1] * k1[rows, :] + res[2] * k2[rows, :] + res[3] * k3[rows, :]
        resid[:, cols] = left.T


def f32(*shape):
    return jax.ShapeDtypeStruct(shape, F32)


def on_device(
    load_cases,
    initial,
    dual_blocks,
    dirichlet,
    rigid_modes,
    coarse_inverse,
    face_block,
    active,
    membership,
):
    own_index = lax.axis_index("sub")
    my_group = lax.dynamic_slice_in_dim(membership, own_index, 1)
    group = (membership == my_group).astype(F32)[None, :]
    gates = active.astype(F32)
    terms = pltpu.VMEM((M, 2 * K), BF16)
    pieces = pltpu.VMEM((PER_CLU * E, 2 * K), BF16)
    vec, face = f32(M, K), f32(FACE, K)
    big = 2 * M * M * 2 * K

    def swap(faces):
        got = []
        for colour in range(NCOL - 1):
            pairs = [(s, s ^ (1 << colour)) for s in range(CLU)]
            got.append(lax.ppermute(faces[colour], "clu", pairs))
        pairs = [(s, s ^ 1) for s in range(PER_CLU)]
        got.append(lax.ppermute(faces[3], "sub", pairs))
        return got

    def spread(value, axis):
        return lax.all_to_all(value, axis, 0, 0, tiled=True)

    stacked, correct, inv_terms = call(
        prep_body,
        [
            jax.ShapeDtypeStruct((2 * E, M), BF16),
            jax.ShapeDtypeStruct((M, 4 * E), BF16),
            jax.ShapeDtypeStruct((2 * E, PER_CLU * E), BF16),
        ],
        [SMEM, VMEM, VMEM],
        moved=2 << 20,
    )(face_block, rigid_modes, coarse_inverse)

    faces = call(
        first_body, [face] * 4, [SMEM, VMEM, VMEM], [terms], flops=big, moved=6 << 20
    )(face_block, initial, dual_blocks)
    got = swap(faces)
    w, sent = call(
        asm_first_body,
        [vec, f32(PER_CLU, E, K)],
        [SMEM, SMEM] + [VMEM] * 10,
        [terms],
        flops=big // 12,
        moved=4 << 20,
    )(face_block, gates, *faces, *got, stacked, load_cases)

    vectors = []
    for stage in range(2 * ITERS):
        op = dual_blocks if stage % 2 else dirichlet
        v, *faces = call(
            mat_body,
            [vec] + [face] * 4,
            [SMEM, SMEM] + [VMEM] * 5,
            [terms, pieces],
            flops=big,
            moved=8 << 20,
        )(face_block, group, w, spread(sent, "sub"), inv_terms, correct, op)
        vectors.append(v)
        got = swap(faces)
        w, sent = call(
            asm_body,
            [vec, f32(PER_CLU, E, K)],
            [SMEM] + [VMEM] * 9,
            [terms],
            flops=big // 12,
            moved=3 << 20,
        )(gates, *faces, *got, stacked)
    bases, searches = vectors[0::2], vectors[1::2]
    last, sums = call(
        gram_body,
        [vec, f32(CLU, ROWS, K)],
        [SMEM] + [VMEM] * 7,
        [pieces],
        flops=big // 12,
        moved=5 << 20,
    )(group, w, spread(sent, "sub"), inv_terms, correct, *bases)
    (sums,) = call(combine_body, [f32(PER_CLU, ROWS, K)], [VMEM], moved=1 << 19)(spread(sums, "clu"))
    return tuple(
        call(last_body, [f32(K, M), f32(K, M)], [SMEM] + [VMEM] * 9, moved=8 << 20)(
            face_block, spread(sums, "sub"), initial, *searches, *bases, last
        )
    )


def solution(mesh):
    in_specs = (
        P(None, ("clu", "sub")),
        P(None, ("clu", "sub")),
        P(("clu", "sub"), None),
        P(("clu", "sub"), None),
        P(("clu", "sub"), None),
        P(("clu", "sub"), None),
        P(("clu", "sub"), None),
        P(("clu", "sub"), None),
        P("clu"),
    )
    out_specs = (P(None, ("clu", "sub")), P(None, ("clu", "sub")))
    return jax.shard_map(
        on_device, mesh=mesh, in_specs=in_specs, out_specs=out_specs, check_vma=False
    )
```

```python
import functools

import jax
import jax.numpy as jnp
from jax import lax
from jax.experimental import pallas as pl
from jax.experimental.pallas import tpu as pltpu
from jax.sharding import PartitionSpec as P


BLK = 128
E = 64
K = 128
M = 1536
NB = 12
NCOL = 4
SLOTS = 3
FACE = SLOTS * BLK
ITERS = 3
PER_CLU = 8
CLU = 32
ROWS = 16
PAIRS = ((0, 1), (0, 2), (0, 3), (1, 1), (1, 2), (1, 3), (2, 2), (2, 3), (3, 3))


F32 = jnp.float32
BF16 = jnp.bfloat16
VMEM = pl.BlockSpec(memory_space=pltpu.VMEM)
SMEM = pl.BlockSpec(memory_space=pltpu.SMEM)


def call(body, outs, in_specs, scratch=(), limit=24, flops=0, moved=0):
    return pl.pallas_call(
        body,
        out_shape=outs,
        in_specs=in_specs,
        out_specs=[VMEM] * len(outs),
        scratch_shapes=list(scratch),
        compiler_params=pltpu.CompilerParams(vmem_limit_bytes=limit << 20),
        cost_estimate=pl.CostEstimate(flops=flops, bytes_accessed=moved, transcendentals=0),
    )


def split(x):
    hi = x.astype(BF16)
    return hi, (x - hi.astype(F32)).astype(BF16)


def dot(a, b):
    return jnp.dot(a, b, preferred_element_type=F32)


def three(out):
    return out[:E, :K] + out[:E, K:] + out[E:, :K]


def block(index):
    return pl.ds(pl.multiple_of(index * BLK, BLK), BLK)


def put_terms(terms, where, x):
    hi, lo = split(x)
    terms[where, :K] = hi
    terms[where, K:] = lo


def product(fb, op, terms, faces):
    for j in range(NB):
        out = dot(op[block(fb[0, j]), :], terms[...])
        lo = (j % SLOTS) * BLK
        faces[j // SLOTS][lo : lo + BLK, :] = out[:, :K] + out[:, K:]


def prep_body(fb, member, modes, inverse, stacked, correct, inv_terms):
    for j in range(NB):
        hi, lo = split(modes[:, block(fb[0, j])])
        cols = slice(j * BLK, (j + 1) * BLK)
        stacked[:E, cols] = hi
        stacked[E:, cols] = lo
        four = jnp.concatenate([hi, hi, lo, lo], axis=0)
        correct[cols, :] = four.astype(F32).T.astype(BF16)
    mine = member[lax.axis_index("sub")]
    owner = lax.broadcasted_iota(jnp.int32, (E, PER_CLU * E), 1) // E
    keep = jnp.zeros((E, PER_CLU * E), F32)
    for t in range(PER_CLU):
        same = (member[t] == mine).astype(F32)
        keep = jnp.where(owner == t, same, keep)
    hi, lo = split(inverse[...] * keep)
    inv_terms[:E, :] = hi
    inv_terms[E:, :] = lo


def turn_body(start, terms):
    for i in range(NB):
        rows = slice(i * BLK, (i + 1) * BLK)
        put_terms(terms, rows, start[:, rows].T)


def first_body(fb, terms, op, f0, f1, f2, f3):
    product(fb, op, terms, (f0, f1, f2, f3))


def coeffs_out(terms, stacked, sent):
    coeffs = three(dot(stacked[...], terms[...]))
    for t in range(PER_CLU):
        sent[t] = coeffs


def gathered(gates, faces, rcvs, j):
    lo = (j % SLOTS) * BLK
    g = j // SLOTS
    return faces[g][lo : lo + BLK, :] + gates[0, g] * rcvs[g][lo : lo + BLK, :]


def asm_body(gates, f0, f1, f2, f3, r0, r1, r2, r3, stacked, w, sent, terms):
    for j in range(NB):
        rows = slice(j * BLK, (j + 1) * BLK)
        value = gathered(gates, (f0, f1, f2, f3), (r0, r1, r2, r3), j)
        w[rows, :] = value
        put_terms(terms, rows, value)
    coeffs_out(terms, stacked, sent)


def asm_first_body(fb, gates, f0, f1, f2, f3, r0, r1, r2, r3, stacked, load, ahead, w, sent, terms):
    for j in range(NB):
        rows = slice(j * BLK, (j + 1) * BLK)
        value = load[:, block(fb[0, j])].T - gathered(gates, (f0, f1, f2, f3), (r0, r1, r2, r3), j)
        w[rows, :] = value
        put_terms(terms, rows, value)
    coeffs_out(terms, stacked, sent)


def amounts(got, inv_terms, pieces):
    for t in range(PER_CLU):
        put_terms(pieces, slice(t * E, (t + 1) * E), got[t])
    hi, lo = split(three(dot(inv_terms[...], pieces[...])))
    return jnp.concatenate([hi, lo, hi, lo], axis=0)


def mat_body(fb, w, got, inv_terms, correct, op, v, f0, f1, f2, f3, terms, pieces):
    z = amounts(got, inv_terms, pieces)
    for j in range(NB):
        rows = slice(j * BLK, (j + 1) * BLK)
        value = w[rows, :] - dot(correct[rows, :], z)
        v[rows, :] = value
        put_terms(terms, block(fb[0, j]), value)
    product(fb, op, terms, (f0, f1, f2, f3))


def gram_body(w, got, inv_terms, correct, k0, k1, k2, k3, sums, pieces):
    z = amounts(got, inv_terms, pieces)
    tops = [jnp.zeros((8, K), F32) for _ in range(4)]

    def octets(x):
        return x.reshape(BLK // 8, 8, K)

    for j in range(NB):
        rows = slice(j * BLK, (j + 1) * BLK)
        value = w[rows, :] - dot(correct[rows, :], z)
        k3[rows, :] = value
        basis = (k0[rows, :], k1[rows, :], k2[rows, :], value)
        tops = [jnp.maximum(t, jnp.max(octets(jnp.abs(x)), axis=0)) for t, x in zip(tops, basis)]
    tops = [jnp.max(t, axis=0, keepdims=True) for t in tops]
    scales = [jnp.where(t > 1e-37, 1.0 / t, 0.0) for t in tops]
    totals = [jnp.zeros((8, K), F32) for _ in PAIRS]
    for j in range(NB):
        rows = slice(j * BLK, (j + 1) * BLK)
        basis = [x[rows, :] * s for x, s in zip((k0, k1, k2, k3), scales)]
        totals = [t + jnp.sum(octets(basis[a] * basis[b]), axis=0) for t, (a, b) in zip(totals, PAIRS)]
    lines = tops + [jnp.sum(t, axis=0, keepdims=True) for t in totals]
    lines = lines + [jnp.zeros((1, K), F32)] * (ROWS - len(lines))
    table = jnp.concatenate(lines, axis=0)
    for t in range(CLU):
        sums[t] = table


def combine(parts, count):
    tables = [parts[t] for t in range(count)]
    top = functools.reduce(jnp.maximum, tables)[:4]
    scale = jnp.where(top > 1e-37, 1.0 / top, 0.0)
    total = [jnp.zeros((1, K), F32) for _ in PAIRS]
    for table in tables:
        part = table[:4] * scale
        total = [
            t + table[4 + i : 5 + i] * (part[a : a + 1] * part[b : b + 1])
            for i, (t, (a, b)) in enumerate(zip(total, PAIRS))
        ]
    return [top[i : i + 1] for i in range(4)], total


def combine_body(parts, sums):
    tops, totals = combine(parts, CLU)
    lines = tops + totals
    lines = lines + [jnp.zeros((1, K), F32)] * (ROWS - len(lines))
    table = jnp.concatenate(lines, axis=0)
    for t in range(PER_CLU):
        sums[t] = table


def last_body(fb, parts, start, t0, t1, t2, k0, k1, k2, k3, mult, resid):
    tops, totals = combine(parts, PER_CLU)
    gram = {}
    for total, (a, b) in zip(totals, PAIRS):
        gram[a, b] = gram[b, a] = total
    inv = [jnp.where(t > 1e-37, 1.0 / t, 0.0) for t in tops]
    ratio = [tops[j + 1] * inv[j] for j in range(3)]
    zero = jnp.zeros((1, K), F32)
    res = [tops[0], zero, zero, zero]
    mul = [zero, zero, zero]
    for i in range(ITERS):
        img = [zero] + [res[j] * ratio[j] for j in range(3)]
        cross, image = zero, zero
        for b in range(1, i + 2):
            for a in range(i + 1):
                cross = cross + (res[a] * img[b]) * gram[a, b]
            for a in range(1, i + 2):
                image = image + (img[a] * img[b]) * gram[a, b]
        step = cross / (image + 1e-06)
        mul = [m + step * (r * s) for m, r, s in zip(mul, res, inv)]
        res = [r - step * q for r, q in zip(res, img)]
    res = [r * s for r, s in zip(res, inv)]
    for j in range(NB):
        rows = slice(j * BLK, (j + 1) * BLK)
        cols = block(fb[0, j])
        gain = mul[0] * t0[rows, :] + mul[1] * t1[rows, :] + mul[2] * t2[rows, :]
        mult[:, cols] = start[:, cols] + gain.T
        left = res[0] * k0[rows, :] + res[1] * k1[rows, :] + res[2] * k2[rows, :] + res[3] * k3[rows, :]
        resid[:, cols] = left.T


def f32(*shape):
    return jax.ShapeDtypeStruct(shape, F32)


def on_device(
    load_cases,
    initial,
    dual_blocks,
    dirichlet,
    rigid_modes,
    coarse_inverse,
    face_block,
    active,
    membership,
):
    gates = active.astype(F32)
    terms = pltpu.VMEM((M, 2 * K), BF16)
    pieces = pltpu.VMEM((PER_CLU * E, 2 * K), BF16)
    vec, face = f32(M, K), f32(FACE, K)
    big = 2 * M * M * 2 * K

    def swap(faces):
        got = []
        for colour in range(NCOL):
            axis, bit, count = ("clu", 1 << colour, CLU) if colour < 3 else ("sub", 1, PER_CLU)
            got.append(lax.ppermute(faces[colour], axis, [(s, s ^ bit) for s in range(count)]))
        return got

    def spread(value, axis):
        return lax.all_to_all(value, axis, 0, 0, tiled=True)

    stacked, correct, inv_terms = call(
        prep_body,
        [
            jax.ShapeDtypeStruct((2 * E, M), BF16),
            jax.ShapeDtypeStruct((M, 4 * E), BF16),
            jax.ShapeDtypeStruct((2 * E, PER_CLU * E), BF16),
        ],
        [SMEM, SMEM, VMEM, VMEM],
        moved=2 << 20,
    )(face_block, membership, rigid_modes, coarse_inverse)

    (turned,) = call(
        turn_body, [jax.ShapeDtypeStruct((M, 2 * K), BF16)], [VMEM], flops=K * M, moved=2 << 20
    )(initial)
    faces = call(first_body, [face] * 4, [SMEM, VMEM, VMEM], flops=big, moved=6 << 20)(
        face_block, turned, dual_blocks
    )
    got = swap(faces)
    w, sent = call(
        asm_first_body,
        [vec, f32(PER_CLU, E, K)],
        [SMEM, SMEM] + [VMEM] * 11,
        [terms],
        flops=big // 12,
        moved=4 << 20,
    )(face_block, gates, *faces, *got, stacked, load_cases, dirichlet)

    vectors = []
    for stage in range(2 * ITERS):
        op = dual_blocks if stage % 2 else dirichlet
        v, *faces = call(
            mat_body,
            [vec] + [face] * 4,
            [SMEM] + [VMEM] * 5,
            [terms, pieces],
            flops=big,
            moved=8 << 20,
        )(face_block, w, spread(sent, "sub"), inv_terms, correct, op)
        vectors.append(v)
        got = swap(faces)
        w, sent = call(
            asm_body,
            [vec, f32(PER_CLU, E, K)],
            [SMEM] + [VMEM] * 9,
            [terms],
            flops=big // 12,
            moved=3 << 20,
        )(gates, *faces, *got, stacked)
    bases, searches = vectors[0::2], vectors[1::2]
    last, sums = call(
        gram_body,
        [vec, f32(CLU, ROWS, K)],
        [VMEM] * 7,
        [pieces],
        flops=big // 12,
        moved=5 << 20,
    )(w, spread(sent, "sub"), inv_terms, correct, *bases)
    (sums,) = call(combine_body, [f32(PER_CLU, ROWS, K)], [VMEM], moved=1 << 19)(spread(sums, "clu"))
    return tuple(
        call(last_body, [f32(K, M), f32(K, M)], [SMEM] + [VMEM] * 9, moved=8 << 20)(
            face_block, spread(sums, "sub"), initial, *searches, *bases, last
        )
    )


def solution(mesh):
    in_specs = (
        P(None, ("clu", "sub")),
        P(None, ("clu", "sub")),
        P(("clu", "sub"), None),
        P(("clu", "sub"), None),
        P(("clu", "sub"), None),
        P(("clu", "sub"), None),
        P(("clu", "sub"), None),
        P(("clu", "sub"), None),
        P("clu"),
    )
    out_specs = (P(None, ("clu", "sub")), P(None, ("clu", "sub")))
    return jax.shard_map(
        on_device, mesh=mesh, in_specs=in_specs, out_specs=out_specs, check_vma=False
    )
```
